128 devices in a mesh: oi: 8 (over x, z_lo), oj: 16 (over z_hi, y, core).
Axes of the slice: x: 4, y: 4, z: 4 (z_hi: 2, z_lo: 2; z = z_hi * 2 + z_lo), core: 2. Of those that a mesh axis runs over, the one named last changes fastest.
Arguments:
- amplitudes: bfloat16 [256, 256, 1024], P('oj', 'oi'), may hold values from -0.15625 to 0.15625
- exchange_ints: bfloat16 [256, 256, 1024], P('oj', 'oi'), may hold values from -6 to 6
- hole_factors: bfloat16 [1024, 1024], P(('oi', 'oj')), may hold values from -4 to 4
- occ_energy: float32 [32], replicated, may hold values from -2 to -0.5
- vir_energy: float32 [256], replicated, may hold values from 0.2 to 3
Outputs:
- amplitude_update: float32 [256, 256, 1024], P('oj', None, 'oi')
The draws below stay inside these ranges and needn't reach their ends.
All inputs are finite; a program needn't handle non-finite values.
Results may differ from the reference program's by a relative error of at most 0.0039.
Values may be sent and summed in bfloat16 or wider, within the bound.
No kernel may reach another device: no remote copies, remote signals or barrier semaphores. Data moves between devices by JAX's collectives and lax.ppermute only.
A program may use at most 128 MiB of HBM per device.

```python
import math
import jax
import jax.numpy as jnp
from jax import lax

O = 32
V = 256
NAUX = 1024


def shard_levels(own_key, shape, split, low, top_value):
    gain, own = 1.0, jax.random.fold_in(own_key, 6)
    for dim, shards_of in split:
        steps = jnp.exp(jax.random.uniform(jax.random.fold_in(own, dim), (shards_of,), jnp.float32, low / len(split), top_value / len(split)))
        gain = gain * jnp.repeat(steps, shape[dim] // shards_of).reshape([-1 if axis == dim else 1 for axis in range(len(shape))])
    return gain


def gaussian(stream_key, extent, scale, most, cuts=(), dtype=jnp.bfloat16):
    level = shard_levels(stream_key, extent, cuts, -0.22, 0.18) if cuts else 1.0
    values = jax.random.normal(stream_key, extent, jnp.float32) * scale * level
    return jnp.minimum(jnp.maximum(values, -most), most).astype(dtype)


def setup_inputs(seed: int = 0) -> dict:
    splits = jax.random.split(jax.random.key(seed), 6)
    return {
        "amplitudes": gaussian(splits[0], (V, V, O * O), ((O * V) ** -0.5), 0.15625, ((0, 16), (1, 8))),
        "exchange_ints": gaussian(splits[1], (V, V, O * O), 1.0, 6.0, ((0, 16), (1, 8))),
        "hole_factors": gaussian(splits[2], (NAUX, O * O), (V ** 0.25 * (O * NAUX) ** -0.25), 4.0, ((0, 128),)),
        "occ_energy": jnp.clip(jax.random.uniform(splits[3], (O,), jnp.float32, -2.0, -0.5), -2.0, -0.5),
        "vir_energy": jnp.clip(jnp.exp(jax.random.uniform(splits[4], (V,), jnp.float32, math.log(0.2), math.log(3.0))), 0.2, 3.0),
    }


def reference(amplitudes, exchange_ints, hole_factors, occ_energy, vir_energy):
    amp_matrix = amplitudes.reshape(V * V, O * O)
    ints_matrix = exchange_ints.reshape(V * V, O * O)
    factors = hole_factors.astype(jnp.float32).reshape(NAUX, O, O)
    density = jnp.einsum('pik,pjl->ijkl', factors, factors).reshape(O * O, O * O)
    quadratic = lax.dot_general(amp_matrix, ints_matrix, (((0,), (0,)), ((), ())), preferred_element_type=jnp.float32)
    hole_ints = (density + quadratic).astype(jnp.bfloat16)
    ladder = lax.dot_general(amp_matrix, hole_ints, (((1,), (1,)), ((), ())), preferred_element_type=jnp.float32)
    partial_value = (ladder + ints_matrix.astype(jnp.float32)).astype(jnp.bfloat16).reshape(V, V, O, O)
    mirror = jnp.transpose(partial_value, (1, 0, 3, 2)).astype(jnp.float32)
    summed_pair = partial_value.astype(jnp.float32) + mirror
    denominator = (vir_energy[:, None, None, None] + vir_energy[None, :, None, None]
                   - occ_energy[None, None, :, None] - occ_energy[None, None, None, :])
    return (summed_pair / denominator).reshape(V, V, O * O)
```

```python
import functools

import jax
import jax.numpy as jnp
from jax import lax
from jax.experimental import pallas as pl
from jax.experimental.pallas import tpu as pltpu
from jax.sharding import Mesh, PartitionSpec as P

BF16, F32 = jnp.bfloat16, jnp.float32
CHIPS = ("x", "y", "zh", "zl")
OI = ("x", "zl")
OJ = ("zh", "y", "c")
ALL = OI + OJ
SWAP = [(0, 1), (1, 0)]
VMEM_LIMIT = 48 * 1024 * 1024


def params():
    return pltpu.CompilerParams(vmem_limit_bytes=VMEM_LIMIT)


def quad_kernel(core, amp_own, amp_peer, ints_own, ints_peer, fac, out, left, right, acc):
    step = pl.program_id(0)

    @pl.when(step == 0)
    def _():
        row = lax.broadcasted_iota(jnp.int32, (32, 1024), 0)
        col = lax.broadcasted_iota(jnp.int32, (32, 1024), 1)
        pick_k = (row == col // 32).astype(F32).astype(BF16)
        pick_l = (row == col % 32).astype(F32).astype(BF16)
        left[...] = jnp.dot(fac[...], pick_k, preferred_element_type=F32)
        right[...] = jnp.dot(fac[...], pick_l, preferred_element_type=F32)

    dims = (((0,), (0,)), ((), ()))
    acc[...] = lax.dot_general(
        amp_own[...], ints_own[...], dims, preferred_element_type=F32
    ) + lax.dot_general(amp_peer[...], ints_peer[...], dims, preferred_element_type=F32)

    def one(ii, carry):
        first = core[0] * 16 + step * 4 + ii
        rows = pl.ds(pl.multiple_of(ii * 32, 32), 32)
        total = acc[rows, :]
        for p in range(16):
            total = total + left[pl.ds(p * 32 + first, 1), :] * right[p * 32 : p * 32 + 32, :]
        out[rows, :] = total.astype(BF16)
        return carry

    lax.fori_loop(0, 4, one, 0)


def sum_kernel(parts, out):
    total = jnp.sum(parts[...].astype(F32), axis=0).astype(BF16)
    out[...] = jnp.broadcast_to(total[None], out.shape)


def ladder_kernel(core, amp, own, peer, ints, out):
    mine = pl.program_id(0) // 4 == core[0]
    rows = jnp.where(mine, own[...], peer[...])
    total = lax.dot_general(
        amp[...], rows, (((1,), (1,)), ((), ())), preferred_element_type=F32
    )
    out[0] = (total + ints[...].astype(F32)).astype(BF16)


def spread_kernel(part, perm, out, wide):
    for r in range(8):
        for ob in range(2):
            for ah in range(2):
                base = ((r * 2 + ob) * 2 + ah) * 16
                for al in range(8):
                    wide[base : base + 16, al * 128 : al * 128 + 128] = part[
                        r, ah * 8 + al, ob * 16 : ob * 16 + 16, :
                    ]
    for q in range(8):
        moved = jnp.dot(
            wide[...], perm[:, q * 128 : q * 128 + 128], preferred_element_type=F32
        )
        out[q] = moved.astype(BF16).reshape(16, 32, 128)


def final_kernel(place, occ, vir, part, mirror, perm, virb, out, wide):
    for q in range(8):
        wide[:, q * 128 : q * 128 + 128] = mirror[q].reshape(512, 128)
    for al in range(8):
        moved = jnp.dot(
            wide[...], perm[:, al * 128 : al * 128 + 128], preferred_element_type=F32
        )
        for o in range(16):
            for ah in range(2):
                base = (o * 2 + ah) * 16
                out[pl.ds(o * 16 + ah * 8 + al, 16, stride=256), :] = moved[base : base + 16, :]
    lane = lax.broadcasted_iota(jnp.int32, (8, 128), 1)
    first = jnp.zeros((8, 128), F32)
    second = jnp.zeros((8, 128), F32)
    for i in range(4):
        first = jnp.where(lane // 32 == i, occ[place[0] * 4 + i], first)
    for j in range(32):
        second = jnp.where(lane % 32 == j, occ[j], second)
    first, second = first[:1], second[:1]

    def one(a, carry):
        energy = vir[place[1] * 16 + a]
        for r in range(8):
            rows = pl.ds(pl.multiple_of(a * 256 + r * 32, 32), 32)
            direct = part[r, pl.ds(pl.multiple_of(a * 32, 32), 32), :].astype(F32)
            low = energy + virb[r * 32 : r * 32 + 32, :] - first - second
            out[rows, :] = (direct + out[rows, :]) / low
        return carry

    lax.fori_loop(0, 16, one, 0)


def moves():
    row = lax.broadcasted_iota(jnp.int32, (1024, 1024), 0)
    col = lax.broadcasted_iota(jnp.int32, (1024, 1024), 1)
    high, mid, low = row // 128, row % 128, row % 4
    spread = (mid // 4 % 8) * 128 + high * 16 + (mid // 32) * 4 + low
    gather = (mid // 16) * 128 + low * 32 + high * 4 + mid // 4 % 4
    return (spread == col).astype(BF16), (gather == col).astype(BF16)


def swap_chips(value):
    return lax.all_to_all(value, CHIPS, 0, 0, tiled=False)


def local(amplitudes, exchange_ints, hole_factors, occ_energy, vir_energy):
    core = lax.axis_index("c").astype(jnp.int32).reshape(1)
    place = jnp.stack([lax.axis_index(OI), lax.axis_index(OJ)]).astype(jnp.int32)
    amp = amplitudes.reshape(512, 1024)
    ints = exchange_ints.reshape(512, 1024)
    amp_peer = lax.ppermute(amp, "c", SWAP)
    ints_peer = lax.ppermute(ints, "c", SWAP)
    fac_peer = lax.ppermute(hole_factors, "c", SWAP)
    spread, gather = moves()
    virb = jnp.broadcast_to(vir_energy[:, None], (256, 128))
    factors = jnp.concatenate([hole_factors, fac_peer]).reshape(512, 32)
    whole = lambda shape: pl.BlockSpec(shape, lambda g, s: (0,) * len(shape))
    half_part = pl.pallas_call(
        quad_kernel,
        out_shape=jax.ShapeDtypeStruct((512, 1024), BF16),
        grid_spec=pltpu.PrefetchScalarGridSpec(
            num_scalar_prefetch=1,
            grid=(4,),
            in_specs=[
                pl.BlockSpec((512, 128), lambda g, s: (0, s[0] * 4 + g)),
                pl.BlockSpec((512, 128), lambda g, s: (0, s[0] * 4 + g)),
                whole((512, 1024)),
                whole((512, 1024)),
                whole((512, 32)),
            ],
            out_specs=pl.BlockSpec((128, 1024), lambda g, s: (g, 0)),
            scratch_shapes=[
                pltpu.VMEM((512, 1024), F32),
                pltpu.VMEM((512, 1024), F32),
                pltpu.VMEM((128, 1024), F32),
            ],
        ),
        compiler_params=params(),
        name="quad",
    )(core, amp, amp_peer, ints, ints_peer, factors)
    parts = swap_chips(half_part.reshape(64, 8, 1024))
    vmem = pl.BlockSpec(memory_space=pltpu.VMEM)
    smem = pl.BlockSpec(memory_space=pltpu.SMEM)
    sent = pl.pallas_call(
        sum_kernel,
        out_shape=jax.ShapeDtypeStruct((64, 8, 1024), BF16),
        in_specs=[vmem],
        out_specs=vmem,
        compiler_params=params(),
        name="sum",
    )(parts)
    hole_own = swap_chips(sent).reshape(512, 1024)
    hole_peer = lax.ppermute(hole_own, "c", SWAP)
    chunks = pl.pallas_call(
        ladder_kernel,
        out_shape=jax.ShapeDtypeStruct((8, 512, 128), BF16),
        grid_spec=pltpu.PrefetchScalarGridSpec(
            num_scalar_prefetch=1,
            grid=(8,),
            in_specs=[
                whole((512, 1024)),
                pl.BlockSpec((128, 1024), lambda g, s: (g % 4, 0)),
                pl.BlockSpec((128, 1024), lambda g, s: (g % 4, 0)),
                pl.BlockSpec((512, 128), lambda g, s: (0, g)),
            ],
            out_specs=pl.BlockSpec((1, 512, 128), lambda g, s: (g, 0, 0)),
        ),
        compiler_params=params(),
        name="ladder",
    )(core, amp, hole_own, hole_peer, ints)
    part = lax.all_to_all(chunks, OI, 0, 0, tiled=False)
    outgoing = pl.pallas_call(
        spread_kernel,
        out_shape=jax.ShapeDtypeStruct((8, 16, 32, 128), BF16),
        in_specs=[vmem, vmem],
        out_specs=vmem,
        scratch_shapes=[pltpu.VMEM((512, 1024), BF16)],
        compiler_params=params(),
        name="spread",
    )(part.reshape(8, 16, 32, 128), spread)
    mirror = lax.all_to_all(outgoing.reshape(128, 32, 128), ALL, 0, 0, tiled=False)
    result = pl.pallas_call(
        final_kernel,
        out_shape=jax.ShapeDtypeStruct((4096, 128), F32),
        in_specs=[smem, smem, smem, vmem, vmem, vmem, vmem],
        out_specs=vmem,
        scratch_shapes=[pltpu.VMEM((512, 1024), BF16)],
        compiler_params=params(),
        name="final",
    )(place, occ_energy, vir_energy, part, mirror.reshape(8, 16, 32, 128), gather, virb)
    return result.reshape(16, 256, 128)


def solution(mesh):
    fine = Mesh(mesh.devices.reshape(4, 2, 2, 4, 2), ALL)
    placed = (P(OJ, OI, None), P(OJ, OI, None), P(ALL, None), P(), P())
    return jax.shard_map(
        local, mesh=fine, in_specs=placed, out_specs=P(OJ, None, OI), check_vma=False
    )
```

```python
import jax
import jax.numpy as jnp
from jax import lax
from jax.experimental import pallas as pl
from jax.experimental.pallas import tpu as pltpu
from jax.sharding import Mesh, PartitionSpec as P

BF16, F32 = jnp.bfloat16, jnp.float32
CHIPS = ("x", "y", "zh", "zl")
OI = ("x", "zl")
OJ = ("zh", "y", "c")
ALL = OI + OJ
SWAP = [(0, 1), (1, 0)]
VMEM = pl.BlockSpec(memory_space=pltpu.VMEM)
SMEM = pl.BlockSpec(memory_space=pltpu.SMEM)
ANY = pl.BlockSpec(memory_space=pl.ANY)


def call(kernel, name, outs, ins, out_specs=None, scratch=(), alias=None):
    return pl.pallas_call(
        kernel,
        out_shape=outs,
        in_specs=ins,
        out_specs=out_specs or jax.tree.map(lambda _: VMEM, outs),
        scratch_shapes=list(scratch),
        input_output_aliases=alias or {},
        compiler_params=pltpu.CompilerParams(vmem_limit_bytes=16 * 1024 * 1024),
        name=name,
    )


def shape(dims, dtype=BF16):
    return jax.ShapeDtypeStruct(dims, dtype)


def tables_kernel(place, vir, occ, spread, gather, virb, vira, occ_lanes):
    row = lax.broadcasted_iota(jnp.int32, (128, 128), 0)
    lane = lax.broadcasted_iota(jnp.int32, (128, 128), 1)

    def ones(mask):
        return mask.astype(F32).astype(BF16)

    out_ones = ones(lane % 16 == (row // 32) * 4 + row % 4)
    in_ones = ones(((lane // 32) == row % 4) & (lane % 4 == row // 4 % 4))
    out_rows = [out_ones * ones(row // 4 % 8 == b) for b in range(8)]
    in_rows = [in_ones * ones(row // 16 == b) for b in range(8)]
    for high in range(8):
        rows = slice(high * 128, high * 128 + 128)
        out_lanes = ones(lane // 16 == high)
        in_lanes = ones(lane // 4 % 8 == high)
        for b in range(8):
            cols = slice(b * 128, b * 128 + 128)
            spread[rows, cols] = out_rows[b] * out_lanes
            gather[rows, cols] = in_rows[b] * in_lanes
    for half in range(2):
        cols = slice(half * 128, half * 128 + 128)
        diagonal = jnp.where(row == lane, jnp.broadcast_to(vir[:1, cols], (128, 128)), 0.0)
        virb[cols, :] = jnp.broadcast_to(jnp.sum(diagonal, axis=1, keepdims=True), (128, 128))
    vira[...] = virb[pl.ds(pl.multiple_of(place[1] * 16, 16), 16), :]
    second = occ[...]
    one = lane[:8]
    first = jnp.zeros((8, 128), F32)
    for i in range(4):
        mine = jnp.where(one == place[0] * 4 + i, second, 0.0)
        value = jnp.broadcast_to(jnp.sum(mine, axis=1, keepdims=True), (8, 128))
        first = jnp.where(one // 32 == i, value, first)
    occ_lanes[:8] = first
    occ_lanes[8:] = second


def add_density(core, fac, left, right, start, out):
    row = lax.broadcasted_iota(jnp.int32, (32, 1024), 0)
    col = lax.broadcasted_iota(jnp.int32, (32, 1024), 1)
    pick_k = (row == col // 32).astype(F32).astype(BF16)
    pick_l = (row == col % 32).astype(F32).astype(BF16)
    left[...] = jnp.dot(fac[...], pick_k, preferred_element_type=F32)
    right[...] = jnp.dot(fac[...], pick_l, preferred_element_type=F32)

    def one(i, carry):
        first = core[0] * 16 + i
        rows = pl.ds(pl.multiple_of(i * 32, 32), 32)
        total = left[pl.ds(first, 1), :] * right[:32, :]
        for p in range(1, 8):
            total = total + left[pl.ds(p * 32 + first, 1), :] * right[p * 32 : p * 32 + 32, :]
        out[rows, :] = total if start is None else total + start[rows, :]
        return carry

    lax.fori_loop(0, 16, one, 0)


def quadratic(core, g, amp, ints):
    cols = pl.ds(pl.multiple_of(core[0] * 512 + g * 128, 128), 128)
    return lax.dot_general(
        amp[:, cols], ints[...], (((0,), (0,)), ((), ())), preferred_element_type=F32
    )


def density_kernel(core, fac, out, left, right):
    add_density(core, fac, left, right, None, out)


def own_kernel(core, start, fac, amp, ints, out, left, right, held):
    for g in range(4):
        rows = slice(g * 128, g * 128 + 128)
        held[rows, :] = start[rows, :] + quadratic(core, g, amp, ints)
    add_density(core, fac, left, right, held, out)


def peer_kernel(core, start, amp, ints, out):
    for g in range(4):
        rows = slice(g * 128, g * 128 + 128)
        out[rows, :] = (start[rows, :] + quadratic(core, g, amp, ints)).astype(BF16)


def sum_kernel(parts, out):
    total = jnp.sum(parts[...].astype(F32), axis=0).astype(BF16)
    out[...] = jnp.broadcast_to(total[None], out.shape)


def ladder_kernel(half, amp, hole, ints, *refs):
    out = refs[-1]
    for g in range(2):
        cols = pl.ds(pl.multiple_of(half[0] * 512 + g * 256, 256), 256)
        total = lax.dot_general(
            amp[...],
            hole[g * 256 : g * 256 + 256, :],
            (((1,), (1,)), ((), ())),
            preferred_element_type=F32,
        )
        total = (total + ints[:, cols].astype(F32)).astype(BF16)
        out[half[0] * 4 + g * 2] = total[:, :128]
        out[half[0] * 4 + g * 2 + 1] = total[:, 128:]


def spread_kernel(part, perm, out, wide):
    for r in range(8):
        for ob in range(2):
            for ah in range(2):
                base = ((r * 2 + ob) * 2 + ah) * 16
                for al in range(8):
                    wide[base : base + 16, al * 128 : al * 128 + 128] = part[
                        r, ah * 8 + al, ob * 16 : ob * 16 + 16, :
                    ]
    for q in range(0, 8, 2):
        moved = jnp.dot(
            wide[...], perm[:, q * 128 : q * 128 + 256], preferred_element_type=F32
        ).astype(BF16)
        out[q] = moved[:, :128].reshape(16, 32, 128)
        out[q + 1] = moved[:, 128:].reshape(16, 32, 128)


def final_kernel(part, mirror, perm, virb, vira, occ_lanes, out, wide, held, sems):
    first, second = occ_lanes[:1], occ_lanes[8:9]

    def copy(a, half):
        rows = pl.ds(pl.multiple_of(a * 256 + half * 128, 128), 128)
        return pltpu.make_async_copy(held.at[rows], out.at[rows], sems.at[half * 16 + a])

    for half in range(2):
        mine = slice(half * 256, half * 256 + 256)
        for q in range(8):
            wide[mine, q * 128 : q * 128 + 128] = mirror[q, half * 8 : half * 8 + 8].reshape(256, 128)
        for al in range(0, 8, 2):
            moved = jnp.dot(
                wide[mine, :], perm[:, al * 128 : al * 128 + 256], preferred_element_type=F32
            )
            for o in range(8):
                for ah in range(2):
                    base = (o * 2 + ah) * 16
                    for s in range(2):
                        row = (half * 8 + o) * 16 + ah * 8 + al + s
                        held[pl.ds(row, 16, stride=256), :] = moved[
                            base : base + 16, s * 128 : s * 128 + 128
                        ]

        def one(a, carry):
            energy = vira[pl.ds(a, 1), :]
            for r in range(half * 4, half * 4 + 4):
                rows = pl.ds(pl.multiple_of(a * 256 + r * 32, 32), 32)
                direct = part[r, pl.ds(pl.multiple_of(a * 32, 32), 32), :].astype(F32)
                low = energy + virb[r * 32 : r * 32 + 32, :] - first - second
                held[rows, :] = (direct + held[rows, :]) / low
            copy(a, half).start()
            return carry

        lax.fori_loop(0, 16, one, 0)
    for half in range(2):
        for a in range(16):
            copy(a, half).wait()


def local(amplitudes, exchange_ints, hole_factors, occ_energy, vir_energy):
    core = lax.axis_index("c").astype(jnp.int32).reshape(1)
    place = jnp.stack([lax.axis_index(OI), lax.axis_index(OJ)]).astype(jnp.int32)
    amp = amplitudes.reshape(512, 1024)
    ints = exchange_ints.reshape(512, 1024)
    fac = hole_factors.reshape(256, 32)
    fac_peer = lax.ppermute(fac, "c", SWAP)
    amp_peer = lax.ppermute(amp, "c", SWAP)
    ints_peer = lax.ppermute(ints, "c", SWAP)
    pieces = [pltpu.VMEM((256, 1024), F32)] * 2
    square = shape((512, 1024), F32)
    density = call(density_kernel, "density", square, [SMEM, VMEM], scratch=pieces)(core, fac)
    own = call(own_kernel, "own", square, [SMEM] + [VMEM] * 4, scratch=pieces + [pltpu.VMEM((512, 1024), F32)])(
        core, density, fac_peer, amp, ints
    )
    half_part = call(peer_kernel, "peer", shape((512, 1024)), [SMEM] + [VMEM] * 3)(
        core, own, amp_peer, ints_peer
    )
    parts = lax.all_to_all(half_part.reshape(64, 8, 1024), CHIPS, 0, 0, tiled=False)
    sent = call(sum_kernel, "sum", shape((64, 8, 1024)), [VMEM])(parts)
    hole_own = lax.all_to_all(sent, CHIPS, 0, 0, tiled=False).reshape(512, 1024)
    hole_peer = lax.ppermute(hole_own, "c", SWAP)
    chunks = call(ladder_kernel, "ladder_own", shape((8, 512, 128)), [SMEM] + [VMEM] * 3)(
        core, amp, hole_own, ints
    )
    vir_row = jnp.broadcast_to(vir_energy[None], (8, 256))
    occ_row = jnp.broadcast_to(jnp.tile(occ_energy, 4)[None], (8, 128))
    place, hole_own = lax.optimization_barrier((place, hole_own))
    tables = call(
        tables_kernel,
        "tables",
        (
            shape((1024, 1024)),
            shape((1024, 1024)),
            shape((256, 128), F32),
            shape((16, 128), F32),
            shape((16, 128), F32),
        ),
        [SMEM, VMEM, VMEM],
    )(place, vir_row, occ_row)
    chunks, spread, gather, virb, vira, occ_lanes = lax.optimization_barrier((chunks, *tables))
    chunks = call(
        ladder_kernel, "ladder_peer", shape((8, 512, 128)), [SMEM] + [VMEM] * 4, alias={4: 0}
    )(1 - core, amp, hole_peer, ints, chunks)
    part = lax.all_to_all(chunks, OI, 0, 0, tiled=False)
    outgoing = call(
        spread_kernel,
        "spread",
        shape((8, 16, 32, 128)),
        [VMEM] * 2,
        scratch=[pltpu.VMEM((512, 1024), BF16)],
    )(part.reshape(8, 16, 32, 128), spread)
    mirror = lax.all_to_all(outgoing.reshape(128, 32, 128), ALL, 0, 0, tiled=False)
    result = call(
        final_kernel,
        "final",
        shape((4096, 128), F32),
        [VMEM] * 6,
        out_specs=ANY,
        scratch=[
            pltpu.VMEM((512, 1024), BF16),
            pltpu.VMEM((4096, 128), F32),
            pltpu.SemaphoreType.DMA((32,)),
        ],
    )(part, mirror.reshape(8, 16, 32, 128), gather, virb, vira, occ_lanes)
    return result.reshape(16, 256, 128)


def solution(mesh):
    fine = Mesh(mesh.devices.reshape(4, 2, 2, 4, 2), ALL)
    placed = (P(OJ, OI, None), P(OJ, OI, None), P(ALL, None), P(), P())
    return jax.shard_map(
        local, mesh=fine, in_specs=placed, out_specs=P(OJ, None, OI), check_vma=False
    )
```

```python
import jax
import jax.numpy as jnp
from jax import lax
from jax.experimental import pallas as pl
from jax.experimental.pallas import tpu as pltpu
from jax.sharding import Mesh, PartitionSpec as P

BF16, F32 = jnp.bfloat16, jnp.float32
CHIPS = ("x", "y", "zh", "zl")
OI = ("x", "zl")
OJ = ("zh", "y", "c")
ALL = OI + OJ
SWAP = [(0, 1), (1, 0)]
VMEM = pl.BlockSpec(memory_space=pltpu.VMEM)
SMEM = pl.BlockSpec(memory_space=pltpu.SMEM)
ANY = pl.BlockSpec(memory_space=pl.ANY)


def call(kernel, name, outs, ins, out_specs=None, scratch=(), alias=None):
    return pl.pallas_call(
        kernel,
        out_shape=outs,
        in_specs=ins,
        out_specs=out_specs or jax.tree.map(lambda _: VMEM, outs),
        scratch_shapes=list(scratch),
        input_output_aliases=alias or {},
        compiler_params=pltpu.CompilerParams(vmem_limit_bytes=16 * 1024 * 1024),
        name=name,
    )


def shape(dims, dtype=BF16):
    return jax.ShapeDtypeStruct(dims, dtype)


def tables_kernel(after, spread, gather):
    row = lax.broadcasted_iota(jnp.int32, (128, 128), 0)
    lane = lax.broadcasted_iota(jnp.int32, (128, 128), 1)

    def ones(mask):
        return mask.astype(F32).astype(BF16)

    out_ones = ones(lane % 16 == (row // 32) * 4 + row % 4)
    in_ones = ones(((lane // 32) == row % 4) & (lane % 4 == row // 4 % 4))
    out_rows = [out_ones * ones(row // 4 % 8 == b) for b in range(8)]
    in_rows = [in_ones * ones(row // 16 == b) for b in range(8)]
    for high in range(8):
        rows = slice(high * 128, high * 128 + 128)
        out_lanes = ones(lane // 16 == high)
        in_lanes = ones(lane // 4 % 8 == high)
        for b in range(8):
            cols = slice(b * 128, b * 128 + 128)
            spread[rows, cols] = out_rows[b] * out_lanes
            gather[rows, cols] = in_rows[b] * in_lanes


def energies(first_tile, rows_tile, both, virb, vira, occ_lanes):
    row = lax.broadcasted_iota(jnp.int32, (128, 128), 0)
    lane = lax.broadcasted_iota(jnp.int32, (128, 128), 1)
    for half in range(2):
        cols = slice(half * 128, half * 128 + 128)
        wide = jnp.broadcast_to(both[:1, cols], (128, 128))
        diagonal = jnp.where(row == lane, wide, 0.0)
        virb[cols, :] = jnp.broadcast_to(jnp.sum(diagonal, axis=1, keepdims=True), (128, 128))
    vira[...] = virb[pl.ds(pl.multiple_of(rows_tile[0] * 16, 16), 16), :]
    one = lane[:8]
    second = both[:, 256:]
    second = second + pltpu.roll(second, 32, 1)
    second = second + pltpu.roll(second, 64, 1)
    first = jnp.zeros((8, 128), F32)
    for i in range(4):
        mine = jnp.where(one == first_tile[0] * 4 + i, second, 0.0)
        value = jnp.broadcast_to(jnp.sum(mine, axis=1, keepdims=True), (8, 128))
        first = jnp.where(one // 32 == i, value, first)
    occ_lanes[:8] = first
    occ_lanes[8:] = second


def add_density(core, fac, left, right, start, out):
    row = lax.broadcasted_iota(jnp.int32, (32, 1024), 0)
    col = lax.broadcasted_iota(jnp.int32, (32, 1024), 1)
    pick_k = (row == col // 32).astype(F32).astype(BF16)
    pick_l = (row == col % 32).astype(F32).astype(BF16)
    left[...] = jnp.dot(fac[...], pick_k, preferred_element_type=F32)
    right[...] = jnp.dot(fac[...], pick_l, preferred_element_type=F32)

    def one(i, carry):
        first = core[0] * 16 + i
        rows = pl.ds(pl.multiple_of(i * 32, 32), 32)
        total = left[pl.ds(first, 1), :] * right[:32, :]
        for p in range(1, 8):
            total = total + left[pl.ds(p * 32 + first, 1), :] * right[p * 32 : p * 32 + 32, :]
        out[rows, :] = total if start is None else total + start[rows, :]
        return carry

    lax.fori_loop(0, 16, one, 0)


def quadratic(core, g, amp, ints):
    cols = pl.ds(pl.multiple_of(core[0] * 512 + g * 128, 128), 128)
    return lax.dot_general(
        amp[:, cols], ints[...], (((0,), (0,)), ((), ())), preferred_element_type=F32
    )


def density_kernel(core, fac, out, left, right):
    add_density(core, fac, left, right, None, out)


def own_kernel(core, start, fac, amp, ints, out, left, right, held):
    for g in range(4):
        rows = slice(g * 128, g * 128 + 128)
        held[rows, :] = start[rows, :] + quadratic(core, g, amp, ints)
    add_density(core, fac, left, right, held, out)


def peer_kernel(core, start, amp, ints, out):
    for g in range(4):
        rows = slice(g * 128, g * 128 + 128)
        out[rows, :] = (start[rows, :] + quadratic(core, g, amp, ints)).astype(BF16)


def sum_kernel(parts, out):
    total = jnp.sum(parts[...].astype(F32), axis=0).astype(BF16)
    out[...] = jnp.broadcast_to(total[None], out.shape)


def ladder_kernel(half, amp, hole, ints, *refs):
    out = refs[-1]
    for g in range(2):
        cols = pl.ds(pl.multiple_of(half[0] * 512 + g * 256, 256), 256)
        total = lax.dot_general(
            amp[...],
            hole[g * 256 : g * 256 + 256, :],
            (((1,), (1,)), ((), ())),
            preferred_element_type=F32,
        )
        total = (total + ints[:, cols].astype(F32)).astype(BF16)
        out[half[0] * 4 + g * 2] = total[:, :128]
        out[half[0] * 4 + g * 2 + 1] = total[:, 128:]


def spread_kernel(part, perm, out, wide):
    for r in range(8):
        for ob in range(2):
            for ah in range(2):
                base = ((r * 2 + ob) * 2 + ah) * 16
                for al in range(8):
                    wide[base : base + 16, al * 128 : al * 128 + 128] = part[
                        r, ah * 8 + al, ob * 16 : ob * 16 + 16, :
                    ]
    for q in range(0, 8, 2):
        moved = jnp.dot(
            wide[...], perm[:, q * 128 : q * 128 + 256], preferred_element_type=F32
        ).astype(BF16)
        out[q] = moved[:, :128].reshape(16, 32, 128)
        out[q + 1] = moved[:, 128:].reshape(16, 32, 128)


def final_kernel(part, mirror, perm, virb, vira, occ_lanes, out, wide, held, sems):
    for q in range(8):
        wide[:, q * 128 : q * 128 + 128] = mirror[q].reshape(512, 128)
    for al in range(0, 8, 2):
        moved = jnp.dot(
            wide[...], perm[:, al * 128 : al * 128 + 256], preferred_element_type=F32
        )
        for o in range(16):
            for ah in range(2):
                base = (o * 2 + ah) * 16
                for s in range(2):
                    held[pl.ds(o * 16 + ah * 8 + al + s, 16, stride=256), :] = moved[
                        base : base + 16, s * 128 : s * 128 + 128
                    ]
    first, second = occ_lanes[:1], occ_lanes[8:9]

    def one(a, carry):
        energy = vira[pl.ds(a, 1), :]
        for r in range(8):
            rows = pl.ds(pl.multiple_of(a * 256 + r * 32, 32), 32)
            direct = part[r, pl.ds(pl.multiple_of(a * 32, 32), 32), :].astype(F32)
            low = energy + virb[r * 32 : r * 32 + 32, :] - first - second
            held[rows, :] = (direct + held[rows, :]) / low
        return carry

    copies = []
    for n in range(4):
        lax.fori_loop(n * 4, n * 4 + 4, one, 0)
        rows = slice(n * 1024, n * 1024 + 1024)
        copies.append(pltpu.make_async_copy(held.at[rows], out.at[rows], sems.at[n]))
        copies[-1].start()
    for copy in copies:
        copy.wait()


def local(amplitudes, exchange_ints, hole_factors, occ_energy, vir_energy):
    core = lax.axis_index("c").astype(jnp.int32).reshape(1)
    amp = amplitudes.reshape(512, 1024)
    ints = exchange_ints.reshape(512, 1024)
    fac = hole_factors.reshape(256, 32)
    fac_peer = lax.ppermute(fac, "c", SWAP)
    amp_peer = lax.ppermute(amp, "c", SWAP)
    ints_peer = lax.ppermute(ints, "c", SWAP)
    pieces = [pltpu.VMEM((256, 1024), F32)] * 2
    square = shape((512, 1024), F32)
    both = jnp.concatenate([vir_energy, occ_energy, jnp.zeros((96,), F32)])
    both = jnp.broadcast_to(both[None], (8, 384))
    tiles = [lax.axis_index(a).astype(jnp.int32).reshape(1) for a in (OI, OJ)]
    levels = call(
        energies,
        "energies",
        (shape((256, 128), F32), shape((16, 128), F32), shape((16, 128), F32)),
        [SMEM] * 2 + [VMEM],
    )(*tiles, both)
    fac_here, virb, vira, occ_lanes = lax.optimization_barrier((fac, *levels))
    density = call(density_kernel, "density", square, [SMEM, VMEM], scratch=pieces)(core, fac_here)
    own = call(
        own_kernel,
        "own",
        square,
        [SMEM] + [VMEM] * 4,
        scratch=pieces + [pltpu.VMEM((512, 1024), F32)],
    )(core, density, fac_peer, amp, ints)
    half_part = call(peer_kernel, "peer", shape((512, 1024)), [SMEM] + [VMEM] * 3)(
        core, own, amp_peer, ints_peer
    )
    parts = lax.all_to_all(half_part.reshape(64, 8, 1024), CHIPS, 0, 0, tiled=False)
    sent = call(sum_kernel, "sum", shape((64, 8, 1024)), [VMEM])(parts)
    hole_own = lax.all_to_all(sent, CHIPS, 0, 0, tiled=False).reshape(512, 1024)
    hole_peer = lax.ppermute(hole_own, "c", SWAP)
    chunks = call(ladder_kernel, "ladder_own", shape((8, 512, 128)), [SMEM] + [VMEM] * 3)(
        core, amp, hole_own, ints
    )
    after, hole_own = lax.optimization_barrier((core, hole_own))
    tables = call(tables_kernel, "tables", (shape((1024, 1024)), shape((1024, 1024))), [SMEM])(after)
    chunks, spread, gather = lax.optimization_barrier((chunks, *tables))
    chunks = call(
        ladder_kernel, "ladder_peer", shape((8, 512, 128)), [SMEM] + [VMEM] * 4, alias={4: 0}
    )(1 - core, amp, hole_peer, ints, chunks)
    part = lax.all_to_all(chunks, OI, 0, 0, tiled=False)
    outgoing = call(
        spread_kernel,
        "spread",
        shape((8, 16, 32, 128)),
        [VMEM] * 2,
        scratch=[pltpu.VMEM((512, 1024), BF16)],
    )(part.reshape(8, 16, 32, 128), spread)
    mirror = lax.all_to_all(outgoing.reshape(128, 32, 128), ALL, 0, 0, tiled=False)
    result = call(
        final_kernel,
        "final",
        shape((4096, 128), F32),
        [VMEM] * 6,
        out_specs=ANY,
        scratch=[
            pltpu.VMEM((512, 1024), BF16),
            pltpu.VMEM((4096, 128), F32),
            pltpu.SemaphoreType.DMA((4,)),
        ],
    )(part, mirror.reshape(8, 16, 32, 128), gather, virb, vira, occ_lanes)
    return result.reshape(16, 256, 128)


def solution(mesh):
    fine = Mesh(mesh.devices.reshape(4, 2, 2, 4, 2), ALL)
    placed = (P(OJ, OI, None), P(OJ, OI, None), P(ALL, None), P(), P())
    return jax.shard_map(
        local, mesh=fine, in_specs=placed, out_specs=P(OJ, None, OI), check_vma=False
    )
```

```python
import jax
import jax.numpy as jnp
from jax import lax
from jax.experimental import pallas as pl
from jax.experimental.pallas import tpu as pltpu
from jax.sharding import Mesh, PartitionSpec as P

BF16, F32 = jnp.bfloat16, jnp.float32
CHIPS = ("x", "y", "zh", "zl")
OI = ("x", "zl")
OJ = ("zh", "y", "c")
ALL = OI + OJ
SWAP = [(0, 1), (1, 0)]
VMEM = pl.BlockSpec(memory_space=pltpu.VMEM)
SMEM = pl.BlockSpec(memory_space=pltpu.SMEM)
ANY = pl.BlockSpec(memory_space=pl.ANY)


def call(kernel, name, outs, ins, out_specs=None, scratch=(), alias=None):
    return pl.pallas_call(
        kernel,
        out_shape=outs,
        in_specs=ins,
        out_specs=out_specs or jax.tree.map(lambda _: VMEM, outs),
        scratch_shapes=list(scratch),
        input_output_aliases=alias or {},
        compiler_params=pltpu.CompilerParams(vmem_limit_bytes=16 * 1024 * 1024),
        name=name,
    )


def shape(dims, dtype=BF16):
    return jax.ShapeDtypeStruct(dims, dtype)


def tables_kernel(after, spread, gather):
    row = lax.broadcasted_iota(jnp.int32, (128, 128), 0)
    lane = lax.broadcasted_iota(jnp.int32, (128, 128), 1)

    def ones(mask):
        return mask.astype(F32).astype(BF16)

    out_ones = ones(lane % 16 == (row // 32) * 4 + row % 4)
    in_ones = ones(((lane // 32) == row % 4) & (lane % 4 == row // 4 % 4))
    out_rows = [out_ones * ones(row // 4 % 8 == b) for b in range(8)]
    in_rows = [in_ones * ones(row // 16 == b) for b in range(8)]
    for high in range(8):
        rows = slice(high * 128, high * 128 + 128)
        out_lanes = ones(lane // 16 == high)
        in_lanes = ones(lane // 4 % 8 == high)
        for b in range(8):
            cols = slice(b * 128, b * 128 + 128)
            spread[rows, cols] = out_rows[b] * out_lanes
            gather[rows, cols] = in_rows[b] * in_lanes


def energies(first_tile, rows_tile, both, virb, vira, occ_lanes):
    row = lax.broadcasted_iota(jnp.int32, (128, 128), 0)
    lane = lax.broadcasted_iota(jnp.int32, (128, 128), 1)
    for half in range(2):
        cols = slice(half * 128, half * 128 + 128)
        wide = jnp.broadcast_to(both[:1, cols], (128, 128))
        diagonal = jnp.where(row == lane, wide, 0.0)
        virb[cols, :] = jnp.broadcast_to(jnp.sum(diagonal, axis=1, keepdims=True), (128, 128))
    vira[...] = virb[pl.ds(pl.multiple_of(rows_tile[0] * 16, 16), 16), :]
    one = lane[:8]
    second = both[:, 256:]
    second = second + pltpu.roll(second, 32, 1)
    second = second + pltpu.roll(second, 64, 1)
    first = jnp.zeros((8, 128), F32)
    for i in range(4):
        mine = jnp.where(one == first_tile[0] * 4 + i, second, 0.0)
        value = jnp.broadcast_to(jnp.sum(mine, axis=1, keepdims=True), (8, 128))
        first = jnp.where(one // 32 == i, value, first)
    occ_lanes[:8] = first
    occ_lanes[8:] = second


def add_density(core, fac, left, right, start, out):
    row = lax.broadcasted_iota(jnp.int32, (32, 1024), 0)
    col = lax.broadcasted_iota(jnp.int32, (32, 1024), 1)
    pick_k = (row == col // 32).astype(F32).astype(BF16)
    pick_l = (row == col % 32).astype(F32).astype(BF16)
    left[...] = jnp.dot(fac[...], pick_k, preferred_element_type=F32)
    right[...] = jnp.dot(fac[...], pick_l, preferred_element_type=F32)

    def one(i, carry):
        first = core[0] * 16 + i
        rows = pl.ds(pl.multiple_of(i * 32, 32), 32)
        total = left[pl.ds(first, 1), :] * right[:32, :]
        for p in range(1, 8):
            total = total + left[pl.ds(p * 32 + first, 1), :] * right[p * 32 : p * 32 + 32, :]
        out[rows, :] = total if start is None else total + start[rows, :]
        return carry

    lax.fori_loop(0, 16, one, 0)


def quadratic(core, g, amp, ints):
    cols = pl.ds(pl.multiple_of(core[0] * 512 + g * 128, 128), 128)
    return lax.dot_general(
        amp[:, cols], ints[...], (((0,), (0,)), ((), ())), preferred_element_type=F32
    )


def density_kernel(core, fac, out, left, right):
    add_density(core, fac, left, right, None, out)


def own_kernel(core, start, amp, ints, out):
    for g in range(4):
        rows = slice(g * 128, g * 128 + 128)
        out[rows, :] = start[rows, :] + quadratic(core, g, amp, ints)


def peer_kernel(core, start, fac, amp, ints, out, left, right, held, here, sem):
    copy = pltpu.make_async_copy(ints, here, sem)
    copy.start()
    add_density(core, fac, left, right, start, held)
    copy.wait()
    for g in range(4):
        rows = slice(g * 128, g * 128 + 128)
        out[rows, :] = (held[rows, :] + quadratic(core, g, amp, here)).astype(BF16)


def sum_kernel(parts, out):
    total = jnp.sum(parts[...].astype(F32), axis=0).astype(BF16)
    out[...] = jnp.broadcast_to(total[None], out.shape)


def ladder_kernel(half, amp, hole, ints, *refs):
    out = refs[-1]
    for g in range(2):
        cols = pl.ds(pl.multiple_of(half[0] * 512 + g * 256, 256), 256)
        total = lax.dot_general(
            amp[...],
            hole[g * 256 : g * 256 + 256, :],
            (((1,), (1,)), ((), ())),
            preferred_element_type=F32,
        )
        total = (total + ints[:, cols].astype(F32)).astype(BF16)
        out[half[0] * 4 + g * 2] = total[:, :128]
        out[half[0] * 4 + g * 2 + 1] = total[:, 128:]


def spread_kernel(part, perm, out, wide):
    for r in range(8):
        for ob in range(2):
            for ah in range(2):
                base = ((r * 2 + ob) * 2 + ah) * 16
                for al in range(8):
                    wide[base : base + 16, al * 128 : al * 128 + 128] = part[
                        r, ah * 8 + al, ob * 16 : ob * 16 + 16, :
                    ]
    for q in range(0, 8, 2):
        moved = jnp.dot(
            wide[...], perm[:, q * 128 : q * 128 + 256], preferred_element_type=F32
        ).astype(BF16)
        out[q] = moved[:, :128].reshape(16, 32, 128)
        out[q + 1] = moved[:, 128:].reshape(16, 32, 128)


def final_kernel(part, mirror, perm, virb, vira, occ_lanes, out, wide, held, sems):
    for q in range(8):
        wide[:, q * 128 : q * 128 + 128] = mirror[q].reshape(512, 128)
    for al in range(0, 8, 2):
        moved = jnp.dot(
            wide[...], perm[:, al * 128 : al * 128 + 256], preferred_element_type=F32
        )
        for o in range(16):
            for ah in range(2):
                base = (o * 2 + ah) * 16
                for s in range(2):
                    held[pl.ds(o * 16 + ah * 8 + al + s, 16, stride=256), :] = moved[
                        base : base + 16, s * 128 : s * 128 + 128
                    ]
    first, second = occ_lanes[:1], occ_lanes[8:9]

    def one(a, carry):
        energy = vira[pl.ds(a, 1), :]
        for r in range(8):
            rows = pl.ds(pl.multiple_of(a * 256 + r * 32, 32), 32)
            direct = part[r, pl.ds(pl.multiple_of(a * 32, 32), 32), :].astype(F32)
            low = energy + virb[r * 32 : r * 32 + 32, :] - first - second
            held[rows, :] = (direct + held[rows, :]) / low
        return carry

    copies = []
    for n in range(4):
        lax.fori_loop(n * 4, n * 4 + 4, one, 0)
        rows = slice(n * 1024, n * 1024 + 1024)
        copies.append(pltpu.make_async_copy(held.at[rows], out.at[rows], sems.at[n]))
        copies[-1].start()
    for copy in copies:
        copy.wait()


def local(amplitudes, exchange_ints, hole_factors, occ_energy, vir_energy):
    core = lax.axis_index("c").astype(jnp.int32).reshape(1)
    amp = amplitudes.reshape(512, 1024)
    ints = exchange_ints.reshape(512, 1024)
    fac = hole_factors.reshape(256, 32)
    fac_peer = lax.ppermute(fac, "c", SWAP)
    amp_peer = lax.ppermute(amp, "c", SWAP)
    ints_peer = lax.ppermute(ints, "c", SWAP)
    pieces = [pltpu.VMEM((256, 1024), F32)] * 2
    square = shape((512, 1024), F32)
    both = jnp.concatenate([vir_energy, occ_energy, jnp.zeros((96,), F32)])
    both = jnp.broadcast_to(both[None], (8, 384))
    tiles = [lax.axis_index(a).astype(jnp.int32).reshape(1) for a in (OI, OJ)]
    levels = call(
        energies,
        "energies",
        (shape((256, 128), F32), shape((16, 128), F32), shape((16, 128), F32)),
        [SMEM] * 2 + [VMEM],
    )(*tiles, both)
    fac_here, virb, vira, occ_lanes = lax.optimization_barrier((fac, *levels))
    density = call(density_kernel, "density", square, [SMEM, VMEM], scratch=pieces)(core, fac_here)
    own = call(own_kernel, "own", square, [SMEM] + [VMEM] * 3)(core, density, amp, ints)
    half_part = call(
        peer_kernel,
        "peer",
        shape((512, 1024)),
        [SMEM, VMEM, VMEM, VMEM, ANY],
        scratch=pieces
        + [
            pltpu.VMEM((512, 1024), F32),
            pltpu.VMEM((512, 1024), BF16),
            pltpu.SemaphoreType.DMA(()),
        ],
    )(core, own, fac_peer, amp_peer, ints_peer)
    parts = lax.all_to_all(half_part.reshape(64, 8, 1024), CHIPS, 0, 0, tiled=False)
    sent = call(sum_kernel, "sum", shape((64, 8, 1024)), [VMEM])(parts)
    hole_own = lax.all_to_all(sent, CHIPS, 0, 0, tiled=False).reshape(512, 1024)
    hole_peer = lax.ppermute(hole_own, "c", SWAP)
    chunks = call(ladder_kernel, "ladder_own", shape((8, 512, 128)), [SMEM] + [VMEM] * 3)(
        core, amp, hole_own, ints
    )
    after, hole_own = lax.optimization_barrier((core, hole_own))
    tables = call(tables_kernel, "tables", (shape((1024, 1024)), shape((1024, 1024))), [SMEM])(after)
    chunks, spread, gather = lax.optimization_barrier((chunks, *tables))
    chunks = call(
        ladder_kernel, "ladder_peer", shape((8, 512, 128)), [SMEM] + [VMEM] * 4, alias={4: 0}
    )(1 - core, amp, hole_peer, ints, chunks)
    part = lax.all_to_all(chunks, OI, 0, 0, tiled=False)
    outgoing = call(
        spread_kernel,
        "spread",
        shape((8, 16, 32, 128)),
        [VMEM] * 2,
        scratch=[pltpu.VMEM((512, 1024), BF16)],
    )(part.reshape(8, 16, 32, 128), spread)
    mirror = lax.all_to_all(outgoing.reshape(128, 32, 128), ALL, 0, 0, tiled=False)
    result = call(
        final_kernel,
        "final",
        shape((4096, 128), F32),
        [VMEM] * 6,
        out_specs=ANY,
        scratch=[
            pltpu.VMEM((512, 1024), BF16),
            pltpu.VMEM((4096, 128), F32),
            pltpu.SemaphoreType.DMA((4,)),
        ],
    )(part, mirror.reshape(8, 16, 32, 128), gather, virb, vira, occ_lanes)
    return result.reshape(16, 256, 128)


def solution(mesh):
    fine = Mesh(mesh.devices.reshape(4, 2, 2, 4, 2), ALL)
    placed = (P(OJ, OI, None), P(OJ, OI, None), P(ALL, None), P(), P())
    return jax.shard_map(
        local, mesh=fine, in_specs=placed, out_specs=P(OJ, None, OI), check_vma=False
    )
```

```python
import jax
import jax.numpy as jnp
from jax import lax
from jax.experimental import pallas as pl
from jax.experimental.pallas import tpu as pltpu
from jax.sharding import Mesh, PartitionSpec as P

BF16, F32 = jnp.bfloat16, jnp.float32
CHIPS = ("x", "y", "zh", "zl")
OI = ("x", "zl")
OJ = ("zh", "y", "c")
ALL = OI + OJ
SWAP = [(0, 1), (1, 0)]
VMEM = pl.BlockSpec(memory_space=pltpu.VMEM)
SMEM = pl.BlockSpec(memory_space=pltpu.SMEM)
ANY = pl.BlockSpec(memory_space=pl.ANY)


def call(kernel, name, outs, ins, out_specs=None, scratch=(), alias=None):
    return pl.pallas_call(
        kernel,
        out_shape=outs,
        in_specs=ins,
        out_specs=out_specs or jax.tree.map(lambda _: VMEM, outs),
        scratch_shapes=list(scratch),
        input_output_aliases=alias or {},
        compiler_params=pltpu.CompilerParams(vmem_limit_bytes=16 * 1024 * 1024),
        name=name,
    )


def shape(dims, dtype=BF16):
    return jax.ShapeDtypeStruct(dims, dtype)


def tables_kernel(after, spread, gather):
    row = lax.broadcasted_iota(jnp.int32, (128, 128), 0)
    lane = lax.broadcasted_iota(jnp.int32, (128, 128), 1)

    def ones(mask):
        return mask.astype(F32).astype(BF16)

    out_ones = ones(lane % 16 == (row // 32) * 4 + row % 4)
    in_ones = ones(((lane // 32) == row % 4) & (lane % 4 == row // 4 % 4))
    out_rows = [out_ones * ones(row // 4 % 8 == b) for b in range(8)]
    in_rows = [in_ones * ones(row // 16 == b) for b in range(8)]
    for high in range(8):
        rows = slice(high * 128, high * 128 + 128)
        out_lanes = ones(lane // 16 == high)
        in_lanes = ones(lane // 4 % 8 == high)
        for b in range(8):
            cols = slice(b * 128, b * 128 + 128)
            spread[rows, cols] = out_rows[b] * out_lanes
            gather[rows, cols] = in_rows[b] * in_lanes


def energies(first_tile, rows_tile, both, virb, vira, occ_lanes):
    row = lax.broadcasted_iota(jnp.int32, (128, 128), 0)
    lane = lax.broadcasted_iota(jnp.int32, (128, 128), 1)
    for half in range(2):
        cols = slice(half * 128, half * 128 + 128)
        wide = jnp.broadcast_to(both[:1, cols], (128, 128))
        diagonal = jnp.where(row == lane, wide, 0.0)
        virb[cols, :] = jnp.broadcast_to(jnp.sum(diagonal, axis=1, keepdims=True), (128, 128))
    vira[...] = virb[pl.ds(pl.multiple_of(rows_tile[0] * 16, 16), 16), :]
    one = lane[:8]
    second = both[:, 256:]
    second = second + pltpu.roll(second, 32, 1)
    second = second + pltpu.roll(second, 64, 1)
    first = jnp.zeros((8, 128), F32)
    for i in range(4):
        mine = jnp.where(one == first_tile[0] * 4 + i, second, 0.0)
        value = jnp.broadcast_to(jnp.sum(mine, axis=1, keepdims=True), (8, 128))
        first = jnp.where(one // 32 == i, value, first)
    occ_lanes[:8] = first
    occ_lanes[8:] = second


def add_density(core, fac, left, right, start, out):
    row = lax.broadcasted_iota(jnp.int32, (32, 1024), 0)
    col = lax.broadcasted_iota(jnp.int32, (32, 1024), 1)
    pick_k = (row == col // 32).astype(F32).astype(BF16)
    pick_l = (row == col % 32).astype(F32).astype(BF16)
    left[...] = jnp.dot(fac[...], pick_k, preferred_element_type=F32)
    right[...] = jnp.dot(fac[...], pick_l, preferred_element_type=F32)

    def one(i, carry):
        first = core[0] * 16 + i
        rows = pl.ds(pl.multiple_of(i * 32, 32), 32)
        total = left[pl.ds(first, 1), :] * right[:32, :]
        for p in range(1, 8):
            total = total + left[pl.ds(p * 32 + first, 1), :] * right[p * 32 : p * 32 + 32, :]
        out[rows, :] = total if start is None else total + start[rows, :]
        return carry

    lax.fori_loop(0, 16, one, 0, unroll=2)


def quadratic(core, g, amp, ints):
    cols = pl.ds(pl.multiple_of(core[0] * 512 + g * 128, 128), 128)
    return lax.dot_general(
        amp[:, cols], ints[...], (((0,), (0,)), ((), ())), preferred_element_type=F32
    )


def density_kernel(core, fac, out, left, right):
    add_density(core, fac, left, right, None, out)


def own_kernel(core, start, amp, ints, out):
    for g in range(4):
        rows = slice(g * 128, g * 128 + 128)
        out[rows, :] = start[rows, :] + quadratic(core, g, amp, ints)


def peer_kernel(core, start, fac, amp, ints, out, left, right, held, here, sem):
    copy = pltpu.make_async_copy(ints, here, sem)
    copy.start()
    add_density(core, fac, left, right, start, held)
    copy.wait()
    for g in range(4):
        rows = slice(g * 128, g * 128 + 128)
        out[rows, :] = (held[rows, :] + quadratic(core, g, amp, here)).astype(BF16)


def sum_kernel(parts, out):
    total = jnp.sum(parts[...].astype(F32), axis=0).astype(BF16)
    out[...] = jnp.broadcast_to(total[None], out.shape)


def ladder_kernel(half, amp, hole, ints, *refs):
    out = refs[-1]
    for g in range(2):
        cols = pl.ds(pl.multiple_of(half[0] * 512 + g * 256, 256), 256)
        total = lax.dot_general(
            amp[...],
            hole[g * 256 : g * 256 + 256, :],
            (((1,), (1,)), ((), ())),
            preferred_element_type=F32,
        )
        total = (total + ints[:, cols].astype(F32)).astype(BF16)
        out[half[0] * 4 + g * 2] = total[:, :128]
        out[half[0] * 4 + g * 2 + 1] = total[:, 128:]


def spread_kernel(part, perm, out, wide):
    for r in range(8):
        for ob in range(2):
            for ah in range(2):
                base = ((r * 2 + ob) * 2 + ah) * 16
                for al in range(8):
                    wide[base : base + 16, al * 128 : al * 128 + 128] = part[
                        r, ah * 8 + al, ob * 16 : ob * 16 + 16, :
                    ]
    for q in range(0, 8, 2):
        moved = jnp.dot(
            wide[...], perm[:, q * 128 : q * 128 + 256], preferred_element_type=F32
        ).astype(BF16)
        out[q] = moved[:, :128].reshape(16, 32, 128)
        out[q + 1] = moved[:, 128:].reshape(16, 32, 128)


def final_kernel(part, mirror, perm, virb, vira, occ_lanes, out, wide, held, sems):
    for q in range(8):
        wide[:, q * 128 : q * 128 + 128] = mirror[q].reshape(512, 128)
    for al in range(0, 8, 2):
        moved = jnp.dot(
            wide[...], perm[:, al * 128 : al * 128 + 256], preferred_element_type=F32
        )
        for o in range(16):
            for ah in range(2):
                base = (o * 2 + ah) * 16
                for s in range(2):
                    held[pl.ds(o * 16 + ah * 8 + al + s, 16, stride=256), :] = moved[
                        base : base + 16, s * 128 : s * 128 + 128
                    ]
    first, second = occ_lanes[:1], occ_lanes[8:9]

    def one(a, carry):
        energy = vira[pl.ds(a, 1), :]
        for r in range(8):
            rows = pl.ds(pl.multiple_of(a * 256 + r * 32, 32), 32)
            direct = part[r, pl.ds(pl.multiple_of(a * 32, 32), 32), :].astype(F32)
            low = energy + virb[r * 32 : r * 32 + 32, :] - first - second
            held[rows, :] = (direct + held[rows, :]) / low
        return carry

    copies = []
    for n in range(4):
        lax.fori_loop(n * 4, n * 4 + 4, one, 0)
        rows = slice(n * 1024, n * 1024 + 1024)
        copies.append(pltpu.make_async_copy(held.at[rows], out.at[rows], sems.at[n]))
        copies[-1].start()
    for copy in copies:
        copy.wait()


def local(amplitudes, exchange_ints, hole_factors, occ_energy, vir_energy):
    core = lax.axis_index("c").astype(jnp.int32).reshape(1)
    amp = amplitudes.reshape(512, 1024)
    ints = exchange_ints.reshape(512, 1024)
    fac = hole_factors.reshape(256, 32)
    fac_peer = lax.ppermute(fac, "c", SWAP)
    amp_peer = lax.ppermute(amp, "c", SWAP)
    ints_peer = lax.ppermute(ints, "c", SWAP)
    pieces = [pltpu.VMEM((256, 1024), F32)] * 2
    square = shape((512, 1024), F32)
    both = jnp.concatenate([vir_energy, occ_energy, jnp.zeros((96,), F32)])
    both = jnp.broadcast_to(both[None], (8, 384))
    tiles = [lax.axis_index(a).astype(jnp.int32).reshape(1) for a in (OI, OJ)]
    levels = call(
        energies,
        "energies",
        (shape((256, 128), F32), shape((16, 128), F32), shape((16, 128), F32)),
        [SMEM] * 2 + [VMEM],
    )(*tiles, both)
    fac_here, virb, vira, occ_lanes = lax.optimization_barrier((fac, *levels))
    density = call(density_kernel, "density", square, [SMEM, VMEM], scratch=pieces)(core, fac_here)
    own = call(own_kernel, "own", square, [SMEM] + [VMEM] * 3)(core, density, amp, ints)
    half_part = call(
        peer_kernel,
        "peer",
        shape((512, 1024)),
        [SMEM, VMEM, VMEM, VMEM, ANY],
        scratch=pieces
        + [
            pltpu.VMEM((512, 1024), F32),
            pltpu.VMEM((512, 1024), BF16),
            pltpu.SemaphoreType.DMA(()),
        ],
    )(core, own, fac_peer, amp_peer, ints_peer)
    parts = lax.all_to_all(half_part.reshape(64, 8, 1024), CHIPS, 0, 0, tiled=False)
    sent = call(sum_kernel, "sum", shape((64, 8, 1024)), [VMEM])(parts)
    hole_own = lax.all_to_all(sent, CHIPS, 0, 0, tiled=False).reshape(512, 1024)
    hole_peer = lax.ppermute(hole_own, "c", SWAP)
    chunks = call(ladder_kernel, "ladder_own", shape((8, 512, 128)), [SMEM] + [VMEM] * 3)(
        core, amp, hole_own, ints
    )
    after, hole_own = lax.optimization_barrier((core, hole_own))
    tables = call(tables_kernel, "tables", (shape((1024, 1024)), shape((1024, 1024))), [SMEM])(after)
    chunks, spread, gather = lax.optimization_barrier((chunks, *tables))
    chunks = call(
        ladder_kernel, "ladder_peer", shape((8, 512, 128)), [SMEM] + [VMEM] * 4, alias={4: 0}
    )(1 - core, amp, hole_peer, ints, chunks)
    part = lax.all_to_all(chunks, OI, 0, 0, tiled=False)
    outgoing = call(
        spread_kernel,
        "spread",
        shape((8, 16, 32, 128)),
        [VMEM] * 2,
        scratch=[pltpu.VMEM((512, 1024), BF16)],
    )(part.reshape(8, 16, 32, 128), spread)
    mirror = lax.all_to_all(outgoing.reshape(128, 32, 128), ALL, 0, 0, tiled=False)
    result = call(
        final_kernel,
        "final",
        shape((4096, 128), F32),
        [VMEM] * 6,
        out_specs=ANY,
        scratch=[
            pltpu.VMEM((512, 1024), BF16),
            pltpu.VMEM((4096, 128), F32),
            pltpu.SemaphoreType.DMA((4,)),
        ],
    )(part, mirror.reshape(8, 16, 32, 128), gather, virb, vira, occ_lanes)
    return result.reshape(16, 256, 128)


def solution(mesh):
    fine = Mesh(mesh.devices.reshape(4, 2, 2, 4, 2), ALL)
    placed = (P(OJ, OI, None), P(OJ, OI, None), P(ALL, None), P(), P())
    return jax.shard_map(
        local, mesh=fine, in_specs=placed, out_specs=P(OJ, None, OI), check_vma=False
    )
```
